256 devices in a mesh: ctx: 32 (over x, y, core), head: 8 (over z).
Axes of the slice: x: 4, y: 4, z: 8, core: 2. Of those that a mesh axis runs over, the one named last changes fastest.
Arguments:
- query_rows: bfloat16 [16384, 2048], P('ctx', 'head'), may hold values from -12 to 12
- key_rows: bfloat16 [16384, 2048], P('ctx', 'head'), may hold values from -12 to 12
- value_rows: bfloat16 [16384, 2048], P('ctx', 'head'), may hold values from -6 to 6
- grad_out: bfloat16 [16384, 2048], P('ctx', 'head'), may hold values from -6 to 6
- house_dirs: float32 [128, 2048], P('ctx', 'head'), may hold values from -6 to 6
- owners: int32 [128, 2], P('ctx'), may hold values from 0 to 31, all different within a row; in each aligned block of 4 rows (0 to 3, 4 to 7, ...) at most 2 rows name the same one
- offsets: int32 [128, 2], P('ctx'), may hold values from 0 to 3
- w_query: bfloat16 [4096, 2048], P(None, 'head'), may hold values from -0.09375 to 0.09375
- w_key: bfloat16 [4096, 2048], P(None, 'head'), may hold values from -0.09375 to 0.09375
- w_value: bfloat16 [4096, 2048], P(None, 'head'), may hold values from -0.09375 to 0.09375
Outputs:
- input_grad: bfloat16 [16384, 4096], P('ctx', 'head')
- house_grad: float32 [128, 2048], P('ctx', 'head')
The draws below stay inside these ranges and needn't reach their ends.
Inputs may be any that keep to these rules, and one draw needn't show every extreme that they name: `owners`: each query block names 2 different ctx indices; the query blocks of one ctx index name any one ctx index at most 2 times, and exactly 2 times for some.
All inputs are finite; a program needn't handle non-finite values.
Results may differ from the reference program's by a relative error of at most 0.025.
Values may be sent and summed in bfloat16 or wider, within the bound.
A program may use at most 128 MiB of HBM per device.

```python
import math
import jax
import jax.numpy as jnp
import numpy as np
from jax import lax

D = 4096
HEADS = 16
DH = 128
BLK = 128
MAXL = 2
CAP = 2
BLK_DEV = 4
NB = 128
TOKENS = 16384
HGRP = 2
N_CTX = 32
N_HEAD = 8


def paired_rows(key, which):
    fresh_rows = jax.random.normal(jax.random.fold_in(key, 31 + which), (TOKENS, HEADS * DH), jnp.float32)
    fresh_rows = jnp.clip(fresh_rows, -6.0, 6.0)
    return fresh_rows


def draw_query_rows(key, part):
    return paired_rows(key, 0).astype(jnp.bfloat16)


def draw_key_rows(key, part):
    return paired_rows(key, 1).astype(jnp.bfloat16)


def place_ends(array, rng, least, high):
    longest = array.shape.index(max(array.shape))
    spots = []
    for shift in (0, 1):
        where = [jax.random.randint(jax.random.fold_in(rng, axis), (), 0, length) for axis, length in enumerate(array.shape)]
        where[longest] = (where[longest] + shift) % array.shape[longest]
        spots.append(tuple(where))
    return array.at[spots[0]].set(least).at[spots[1]].set(high)


def steps_of(stream_key, dims, cuts, smallest, largest):
    gain = 1.0
    for dim, parts in cuts:
        steps = jax.random.uniform(jax.random.fold_in(jax.random.fold_in(stream_key, 6), dim), (parts,), jnp.float32, smallest / len(cuts), largest / len(cuts))
        gain = gain * jnp.repeat(jnp.exp(steps), dims[dim] // parts).reshape((-1,) + (1,) * (len(dims) - 1 - dim))
    return gain


def shared_out(key, own, number, rows, amount, top, limit, skew):
    order = jax.random.permutation(key, amount)
    heavy_load, ordinary = portions_of(amount, rows * top, limit, skew, True), portions_of(amount, rows * top, limit, skew, False)
    places = jnp.arange(amount)

    def named(sizes, rotation):
        used = int((sizes > 0).sum())
        fixed = max(1, used // 4)
        moved = fixed + (places - fixed + rotation * (used - fixed)) % max(1, amount - fixed)
        return jnp.zeros((amount,), jnp.int32).at[order[jnp.where(places < fixed, places, moved)]].set(jnp.asarray(sizes, jnp.int32))

    sizes = jnp.where(number % 4 == 0, named(heavy_load, number // 4), named(ordinary, number - number // 4 - 1))
    mixed = jax.random.permutation(jax.random.fold_in(own, 3), amount)
    source_of, taker = mixed[0:amount // 2 * 2:2], mixed[1:amount // 2 * 2:2]
    margin = jnp.minimum(sizes[source_of] - 1, limit - sizes[taker]) // 2
    margin = jnp.where((source_of == order[0]) | (taker == order[0]) | (sizes[taker] == 0), 0, jnp.maximum(margin, 0))
    moved = jax.random.randint(jax.random.fold_in(own, 4), (amount // 2,), 0, 1 << 20) % (margin + 1)
    sizes = sizes.at[source_of].add(-moved).at[taker].add(moved)
    labels = jnp.searchsorted(jnp.cumsum(sizes), jnp.arange(rows * top), side="right").astype(jnp.int32)
    listing = labels.reshape(top, rows).T
    listing = listing[jax.random.permutation(jax.random.fold_in(own, 1), rows)]
    rotation = jax.random.randint(jax.random.fold_in(own, 2), (rows, 1), 0, top)
    return jnp.take_along_axis(listing, (jnp.arange(top)[None, :] + rotation) % top, axis=1)


def portions_of(count, total, bound, skew, full):
    portions = [(1 << 20) // math.isqrt(standing ** skew) + 1 for standing in range(1, count + 1)]
    largest = bound if full else min(bound, max(-(-total // count), total * portions[0] // sum(portions)))
    least = 1 if total - largest >= count - 1 else 0
    counts, rest = [largest] + [least] * (count - 1), total - largest - least * (count - 1)
    while rest > 0:
        movable = [i for i in range(1, count) if counts[i] < largest] or [i for i in range(1, count) if counts[i] < bound]
        whole, remaining = sum([portions[i] for i in movable]), rest
        for i in movable:
            addition = min(bound - counts[i], max(1, remaining * portions[i] // whole), rest)
            counts[i] = counts[i] + addition
            rest = rest - addition
    return np.array(counts)


def centred(rng, shape, width, limit, shards=(), kind=jnp.bfloat16):
    result = width * jax.random.normal(rng, shape, jnp.float32)
    if shards:
        result = result * steps_of(rng, shape, shards, -0.22, 0.18)
    return jnp.clip(result, -limit, limit).astype(kind)


def setup_inputs(seed: int = 0) -> dict:
    key_of = jax.random.split(jax.random.key(seed), 11)
    query_rows = draw_query_rows(jax.random.fold_in(key_of[10], 71), 0)
    key_rows = draw_key_rows(jax.random.fold_in(key_of[10], 71), 0)
    value_rows = centred(key_of[2], (TOKENS, HEADS * DH), 1.0, 6.0, ((0, 32), (1, 8)))
    grad_out = centred(key_of[3], (TOKENS, HEADS * DH), 1.0, 6.0, ((0, 32), (1, 8)))
    house_dirs = centred(key_of[4], (NB, HEADS * DH), 1.0, 6.0, ((0, 32), (1, 8)), jnp.float32)
    owners_keys = jax.random.split(jax.random.fold_in(key_of[5], 1), NB // BLK_DEV)
    owners_turns = jax.random.permutation(jax.random.fold_in(key_of[5], 3), NB // BLK_DEV)
    owners = jax.vmap(lambda own, number: shared_out(jax.random.fold_in(key_of[5], 2), own, number, BLK_DEV, N_CTX, MAXL, CAP, 2))(owners_keys, owners_turns).reshape((NB, MAXL))
    offsets = place_ends(jax.random.randint(key_of[6], (NB, MAXL), 0, BLK_DEV), jax.random.fold_in(key_of[6], 1), 0, BLK_DEV - 1).astype(jnp.int32)
    w_query = centred(key_of[7], (D, HEADS * DH), D ** -0.5, 0.09375, ((1, 8),))
    w_key = centred(key_of[8], (D, HEADS * DH), D ** -0.5, 0.09375, ((1, 8),))
    w_value = centred(key_of[9], (D, HEADS * DH), D ** -0.5, 0.09375, ((1, 8),))
    return dict(query_rows=query_rows, key_rows=key_rows, value_rows=value_rows, grad_out=grad_out, house_dirs=house_dirs, owners=owners, offsets=offsets, w_query=w_query, w_key=w_key, w_value=w_value)


HIGH = lax.Precision.HIGHEST

def narrowed(values_in):
    return lax.optimization_barrier(values_in.astype(jnp.bfloat16)).astype(jnp.float32)

def reflect_apply(unit_dirs, matrices):
    projected = jnp.einsum('hn,hnk->hk', unit_dirs, matrices, precision=HIGH)
    return matrices - 2.0 * unit_dirs[:, :, None] * projected[:, None, :]

def attend(query_blk, key_blk, value_blk, grad_blk, remote_keys, remote_values, scaling):
    block_count, block_rows, head_count, head_size = query_blk.shape
    tok_rows = block_count * block_rows
    query_tok = query_blk.reshape(tok_rows, head_count, head_size)
    key_tok = key_blk.reshape(tok_rows, head_count, head_size)
    value_tok = value_blk.reshape(tok_rows, head_count, head_size)
    grad_tok = grad_blk.reshape(tok_rows, head_count, head_size)
    position = jnp.arange(tok_rows)
    local_scores = jnp.einsum('thd,uhd->htu', query_tok, key_tok) * scaling
    local_scores = jnp.where(position[:, None] >= position[None, :], local_scores, -jnp.inf)
    remote_scores = jnp.einsum('bthd,bkhd->bhtk', query_blk, remote_keys) * scaling

    def to_heads(per_block):
        return per_block.transpose(1, 0, 2).reshape(head_count, tok_rows)

    def to_blocks(per_head):
        return per_head.reshape(head_count, block_count, block_rows).transpose(1, 0, 2)[..., None]
    top_score = jnp.maximum(lax.optimization_barrier(jnp.max(local_scores, axis=2)), to_heads(lax.optimization_barrier(jnp.max(remote_scores, axis=3))))
    exp_total = lax.optimization_barrier(jnp.sum(jnp.exp(local_scores - top_score[:, :, None]), axis=2))
    exp_total = exp_total + to_heads(lax.optimization_barrier(jnp.sum(jnp.exp(remote_scores - to_blocks(top_score)), axis=3)))
    log_total = top_score + jnp.log(exp_total)
    local_probs = jnp.exp(local_scores - log_total[:, :, None])
    remote_probs = jnp.exp(remote_scores - to_blocks(log_total))
    local_pb = narrowed(local_probs)
    remote_pb = narrowed(remote_probs)
    attended = jnp.einsum('htu,uhd->thd', local_pb, value_tok)
    attended = attended + jnp.einsum('bhtk,bkhd->bthd', remote_pb, remote_values).reshape(tok_rows, head_count, head_size)
    delta = lax.optimization_barrier(jnp.sum(grad_tok * attended, axis=2)).T
    local_ds = narrowed(local_probs * (jnp.einsum('thd,uhd->htu', grad_tok, value_tok) - delta[:, :, None]))
    remote_ds = narrowed(remote_probs * (jnp.einsum('bthd,bkhd->bhtk', grad_blk, remote_values) - to_blocks(delta)))
    dq_rot = jnp.einsum('htu,uhd->thd', local_ds, key_tok)
    dq_rot = scaling * (dq_rot + jnp.einsum('bhtk,bkhd->bthd', remote_ds, remote_keys).reshape(tok_rows, head_count, head_size))
    dk_local = scaling * jnp.einsum('htu,thd->uhd', local_ds, query_tok)
    dv_local = jnp.einsum('htu,thd->uhd', local_pb, grad_tok)
    part_key = (scaling * jnp.einsum('bhtk,bthd->bkhd', remote_ds, query_blk)).astype(jnp.bfloat16)
    part_value = jnp.einsum('bhtk,bthd->bkhd', remote_pb, grad_blk).astype(jnp.bfloat16)
    return (dq_rot, dk_local, dv_local, part_key, part_value)

def reference(query_rows, key_rows, value_rows, grad_out, house_dirs, owners, offsets, w_query, w_key, w_value):
    all_blocks = BLK_DEV * N_CTX
    house_heads = house_dirs.reshape(all_blocks, HEADS, DH)
    lengths = jnp.sqrt(lax.optimization_barrier(jnp.sum(house_heads * house_heads, axis=-1, keepdims=True)) + 1e-06)
    unit_dirs = house_heads / lengths
    identity = jnp.broadcast_to(jnp.eye(DH, dtype=jnp.float32), (HEADS, DH, DH))

    def forward(carry, unit_now):
        updated = reflect_apply(unit_now, carry)
        return (updated, updated)
    _, cumulative = lax.scan(forward, identity, unit_dirs)
    query_f32 = query_rows.astype(jnp.float32).reshape(all_blocks, BLK, HEADS, DH)
    key_f32 = key_rows.astype(jnp.float32).reshape(all_blocks, BLK, HEADS, DH)
    query_rot = narrowed(jnp.einsum('bthn,bhnm->bthm', query_f32, cumulative, precision=HIGH))
    key_rot = narrowed(jnp.einsum('bthn,bhnm->bthm', key_f32, cumulative, precision=HIGH))
    value_f32 = value_rows.astype(jnp.float32).reshape(all_blocks, BLK, HEADS, DH)
    grad_f32 = grad_out.astype(jnp.float32).reshape(all_blocks, BLK, HEADS, DH)
    block_ids = (owners * BLK_DEV + offsets).astype(jnp.int32)
    segment_ids = block_ids.reshape(N_CTX, BLK_DEV * MAXL)
    scaling = DH ** (-0.5)

    def by_segment(array_in):
        return array_in.reshape(N_CTX, BLK_DEV, BLK, HEADS, DH)

    def one_segment(inputs):
        query_seg, key_seg, value_seg, grad_seg, listed = inputs
        remote_keys = key_rot[listed].reshape(BLK_DEV, MAXL * BLK, HEADS, DH)
        remote_values = value_f32[listed].reshape(BLK_DEV, MAXL * BLK, HEADS, DH)
        return attend(query_seg, key_seg, value_seg, grad_seg, remote_keys, remote_values, scaling)
    dq_rot, dk_local, dv_local, part_key, part_value = lax.map(one_segment, (by_segment(query_rot), by_segment(key_rot), by_segment(value_f32), by_segment(grad_f32), segment_ids))
    flat_ids = block_ids.reshape(all_blocks * MAXL)
    part_key = lax.optimization_barrier(part_key).astype(jnp.float32).reshape(all_blocks * MAXL, BLK, HEADS, DH)
    part_value = lax.optimization_barrier(part_value).astype(jnp.float32).reshape(all_blocks * MAXL, BLK, HEADS, DH)
    dq_rot = dq_rot.reshape(all_blocks, BLK, HEADS, DH)
    dk_rot = dk_local.reshape(all_blocks, BLK, HEADS, DH) + jax.ops.segment_sum(part_key, flat_ids, num_segments=all_blocks)
    dv_all = dv_local.reshape(all_blocks, BLK, HEADS, DH) + jax.ops.segment_sum(part_value, flat_ids, num_segments=all_blocks)
    dq_out = jnp.einsum('bthm,bhnm->bthn', dq_rot, cumulative, precision=HIGH).astype(jnp.bfloat16).reshape(TOKENS, HEADS * DH)
    dk_out = jnp.einsum('bthm,bhnm->bthn', dk_rot, cumulative, precision=HIGH).astype(jnp.bfloat16).reshape(TOKENS, HEADS * DH)
    dv_out = dv_all.astype(jnp.bfloat16).reshape(TOKENS, HEADS * DH)
    dcum = jnp.einsum('bthn,bthm->bhnm', query_f32, dq_rot, precision=HIGH)
    dcum = dcum + jnp.einsum('bthn,bthm->bhnm', key_f32, dk_rot, precision=HIGH)
    previous = jnp.concatenate([identity[None], cumulative[:-1]], axis=0)

    def backward(carry, inputs):
        dcum_now, unit_now, before = inputs
        adjoint = dcum_now + carry
        dreflect = jnp.einsum('hmn,hkn->hmk', adjoint, before, precision=HIGH)
        return (reflect_apply(unit_now, adjoint), dreflect)
    _, dreflect = lax.scan(backward, jnp.zeros((HEADS, DH, DH), jnp.float32), (dcum, unit_dirs, previous), reverse=True)
    dunit = jnp.einsum('bhmn,bhn->bhm', dreflect, unit_dirs, precision=HIGH)
    dunit = -2.0 * (dunit + jnp.einsum('bhnm,bhn->bhm', dreflect, unit_dirs, precision=HIGH))
    house_grad = (dunit - unit_dirs * lax.optimization_barrier(jnp.sum(unit_dirs * dunit, axis=-1, keepdims=True))) / lengths
    house_grad = house_grad.reshape(all_blocks, HEADS * DH)
    group_width = HGRP * DH
    summed = jnp.zeros((TOKENS, D), jnp.float32)
    for group in range(N_HEAD):
        first = group * group_width
        term = jnp.dot(dq_out[:, first:first + group_width], w_query[:, first:first + group_width].T, preferred_element_type=jnp.float32)
        term = term + jnp.dot(dk_out[:, first:first + group_width], w_key[:, first:first + group_width].T, preferred_element_type=jnp.float32)
        term = term + jnp.dot(dv_out[:, first:first + group_width], w_value[:, first:first + group_width].T, preferred_element_type=jnp.float32)
        summed = summed + narrowed(term)
    return (summed.astype(jnp.bfloat16), house_grad)
```

```python
import jax
import jax.numpy as jnp
from jax import lax
from jax.sharding import PartitionSpec as P

DH = 128
BLK = 128
MAXL = 2

HIGH = lax.Precision.HIGHEST


def reflect_apply(unit_dirs, matrices):
    projected = jnp.einsum("hn,hnk->hk", unit_dirs, matrices, precision=HIGH)
    return matrices - 2.0 * unit_dirs[:, :, None] * projected[:, None, :]


def lower_inverse(gram):
    n = gram.shape[-1]
    row = lax.broadcasted_iota(jnp.int32, (n, n), 0)
    col = lax.broadcasted_iota(jnp.int32, (n, n), 1)
    inv = jnp.broadcast_to(2.0 * jnp.eye(n, dtype=jnp.float32), gram.shape)
    size = 1
    while size < n:
        mask = (row // (2 * size) == col // (2 * size)) & (row // size > col // size)
        part = jnp.where(mask, gram, 0.0)
        inner = jnp.einsum("hij,hjk->hik", part, inv, precision=HIGH)
        inv = inv - lax.optimization_barrier(
            jnp.einsum("hij,hjk->hik", inv, inner, precision=HIGH)
        )
        size *= 2
    return inv


def unit_of(house_heads):
    lengths = jnp.sqrt(jnp.sum(house_heads * house_heads, axis=-1, keepdims=True) + 1e-06)
    return house_heads / lengths, lengths


def shards(
    query_rows, key_rows, value_rows, grad_out, house_dirs, owners, offsets, w_query, w_key, w_value
):
    tok_rows, row_width = query_rows.shape
    head_count = row_width // DH
    block_count = tok_rows // BLK
    entries = block_count * MAXL
    ctx_count = lax.axis_size("ctx")
    my_index = lax.axis_index("ctx")
    all_blocks = ctx_count * block_count
    first = my_index * block_count
    scaling = DH ** (-0.5)
    value_all = lax.all_gather(value_rows, "ctx", axis=0, tiled=True)
    house_all = lax.all_gather(house_dirs, "ctx", axis=0, tiled=True)
    units_all, _ = unit_of(house_all.reshape(all_blocks, head_count, DH).transpose(1, 0, 2))
    house_heads = house_dirs.reshape(block_count, head_count, DH)
    unit_dirs, lengths = unit_of(house_heads)
    gram = jnp.einsum("hin,hjn->hij", units_all, units_all, precision=HIGH)
    solve = lower_inverse(gram)
    k_all = jnp.einsum("hij,hjn->hin", solve, units_all, precision=HIGH)
    ids = jnp.arange(all_blocks)
    below = ids < first
    upto = ids[None, :] < first + jnp.arange(block_count + 1)[:, None]
    identity = jnp.eye(DH, dtype=jnp.float32)
    held = jnp.where(upto[:, None, :, None], units_all[None], 0.0)
    k_each = jnp.broadcast_to(k_all[None], held.shape)
    prods = identity - jnp.einsum("bhin,bhim->bhnm", held, k_each, precision=HIGH)
    previous, cumulative = prods[:-1], prods[1:]
    query_f32 = query_rows.astype(jnp.float32).reshape(block_count, BLK, head_count, DH)
    key_f32 = key_rows.astype(jnp.float32).reshape(block_count, BLK, head_count, DH)
    query_rot = jnp.einsum("bthn,bhnm->bthm", query_f32, cumulative, precision=HIGH).astype(
        jnp.bfloat16
    )
    key_rot = jnp.einsum("bthn,bhnm->bthm", key_f32, cumulative, precision=HIGH).astype(
        jnp.bfloat16
    )
    key_all = lax.all_gather(key_rot.reshape(tok_rows, row_width), "ctx", axis=0, tiled=True)
    entry_ids = (owners * block_count + offsets).reshape(entries)
    remote_keys = key_all.reshape(all_blocks, BLK, row_width)[entry_ids]
    remote_values = value_all.reshape(all_blocks, BLK, row_width)[entry_ids]
    remote_keys = remote_keys.reshape(block_count, MAXL * BLK, head_count, DH)
    remote_values = remote_values.reshape(block_count, MAXL * BLK, head_count, DH)
    query_tok = query_rot.reshape(tok_rows, head_count, DH)
    key_tok = key_rot.reshape(tok_rows, head_count, DH)
    value_tok = value_rows.reshape(tok_rows, head_count, DH)
    grad_tok = grad_out.reshape(tok_rows, head_count, DH)
    grad_blk = grad_out.reshape(block_count, BLK, head_count, DH)
    position = jnp.arange(tok_rows)
    local_scores = (
        jnp.einsum("thd,uhd->htu", query_tok, key_tok, preferred_element_type=jnp.float32) * scaling
    )
    local_scores = jnp.where(position[:, None] >= position[None, :], local_scores, -jnp.inf)
    remote_scores = (
        jnp.einsum("bthd,bkhd->bhtk", query_rot, remote_keys, preferred_element_type=jnp.float32)
        * scaling
    )

    def to_heads(per_block):
        return per_block.transpose(1, 0, 2).reshape(head_count, tok_rows)

    def to_blocks(per_head):
        return per_head.reshape(head_count, block_count, BLK).transpose(1, 0, 2)

    top_score = jnp.maximum(jnp.max(local_scores, axis=2), to_heads(jnp.max(remote_scores, axis=3)))
    exp_total = jnp.sum(jnp.exp(local_scores - top_score[:, :, None]), axis=2)
    exp_total = exp_total + to_heads(
        jnp.sum(jnp.exp(remote_scores - to_blocks(top_score)[..., None]), axis=3)
    )
    log_total = top_score + jnp.log(exp_total)
    log_blocks = to_blocks(log_total)
    local_probs = jnp.exp(local_scores - log_total[:, :, None])
    remote_probs = jnp.exp(remote_scores - log_blocks[..., None])
    local_pb = local_probs.astype(jnp.bfloat16)
    remote_pb = remote_probs.astype(jnp.bfloat16)
    attended = jnp.einsum("htu,uhd->thd", local_pb, value_tok, preferred_element_type=jnp.float32)
    attended = attended + jnp.einsum(
        "bhtk,bkhd->bthd", remote_pb, remote_values, preferred_element_type=jnp.float32
    ).reshape(tok_rows, head_count, DH)
    delta = jnp.sum(grad_tok.astype(jnp.float32) * attended, axis=2).T
    delta_blocks = to_blocks(delta)
    local_dp = jnp.einsum("thd,uhd->htu", grad_tok, value_tok, preferred_element_type=jnp.float32)
    local_ds = (local_probs * (local_dp - delta[:, :, None])).astype(jnp.bfloat16)
    remote_dp = jnp.einsum(
        "bthd,bkhd->bhtk", grad_blk, remote_values, preferred_element_type=jnp.float32
    )
    remote_ds = (remote_probs * (remote_dp - delta_blocks[..., None])).astype(jnp.bfloat16)
    dq_rot = jnp.einsum("htu,uhd->thd", local_ds, key_tok, preferred_element_type=jnp.float32)
    dq_rot = scaling * (
        dq_rot
        + jnp.einsum(
            "bhtk,bkhd->bthd", remote_ds, remote_keys, preferred_element_type=jnp.float32
        ).reshape(tok_rows, head_count, DH)
    )
    dk_local = scaling * jnp.einsum(
        "htu,thd->uhd", local_ds, query_tok, preferred_element_type=jnp.float32
    )
    dv_local = jnp.einsum("htu,thd->uhd", local_pb, grad_tok, preferred_element_type=jnp.float32)
    part_key = (
        scaling
        * jnp.einsum("bhtk,bthd->bkhd", remote_ds, query_rot, preferred_element_type=jnp.float32)
    ).astype(jnp.bfloat16)
    part_value = jnp.einsum(
        "bhtk,bthd->bkhd", remote_pb, grad_blk, preferred_element_type=jnp.float32
    ).astype(jnp.bfloat16)
    pick = (ids[:, None] == entry_ids[None, :]).astype(jnp.bfloat16)

    def give_back(part):
        dense = jnp.einsum(
            "be,erw->brw",
            pick,
            part.reshape(entries, BLK, row_width),
            preferred_element_type=jnp.float32,
        ).astype(jnp.bfloat16)
        return lax.psum_scatter(
            dense.reshape(all_blocks * BLK, row_width), "ctx", scatter_dimension=0, tiled=True
        ).astype(jnp.float32)

    back_values = give_back(part_value)
    back_keys = give_back(part_key)
    dk_rot = (dk_local.reshape(tok_rows, row_width) + back_keys).reshape(
        block_count, BLK, head_count, DH
    )
    dv_out = (dv_local.reshape(tok_rows, row_width) + back_values).astype(jnp.bfloat16)
    dq_rot = dq_rot.reshape(block_count, BLK, head_count, DH)
    dq_out = (
        jnp.einsum("bthm,bhnm->bthn", dq_rot, cumulative, precision=HIGH)
        .astype(jnp.bfloat16)
        .reshape(tok_rows, row_width)
    )
    dk_out = (
        jnp.einsum("bthm,bhnm->bthn", dk_rot, cumulative, precision=HIGH)
        .astype(jnp.bfloat16)
        .reshape(tok_rows, row_width)
    )
    dcum = jnp.einsum("bthn,bthm->bhnm", query_f32, dq_rot, precision=HIGH)
    dcum = dcum + jnp.einsum("bthn,bthm->bhnm", key_f32, dk_rot, precision=HIGH)

    carry = jnp.zeros((head_count, DH, DH), jnp.float32)
    adjoints = [None] * block_count
    for block in range(block_count - 1, -1, -1):
        adjoints[block] = dcum[block] + carry
        carry = reflect_apply(unit_dirs[block], adjoints[block])
    held = below[None, :, None].astype(jnp.float32)
    units_below = units_all * held
    k_below = k_all * held
    through = jnp.einsum("hin,hnm->him", units_below, carry, precision=HIGH)
    to_z = 0.5 * jnp.einsum("hib,him->hbm", solve, through, precision=HIGH)
    crossed = jnp.einsum("hbm,him->hbi", k_below, through, precision=HIGH)
    crossed = jnp.einsum("hbj,hji->hbi", crossed, solve, precision=HIGH)
    crossed = jnp.where(ids[:, None] < ids[None, :], crossed, 0.0)
    to_y = jnp.einsum("hbm,hnm->hbn", k_below, carry, precision=HIGH) - jnp.einsum(
        "hbi,hin->hbn", crossed, units_all, precision=HIGH
    )
    sent = jnp.stack([to_y, to_z], axis=0).transpose(2, 0, 1, 3).reshape(all_blocks, 4 * DH)
    came = lax.psum_scatter(sent, "ctx", scatter_dimension=0, tiled=True)
    came = came.reshape(block_count, 2, head_count, DH)
    adjoint = jnp.stack(adjoints)
    k_own = lax.dynamic_slice_in_dim(k_all, first, block_count, axis=1)
    y_own = came[:, 0] + jnp.einsum("bhnm,hbm->bhn", adjoint, k_own, precision=HIGH)
    z_own = came[:, 1] + jnp.einsum("bhnm,bhn->bhm", adjoint, unit_dirs, precision=HIGH)
    dunit = -2.0 * (0.5 * y_own + jnp.einsum("bhnm,bhm->bhn", previous, z_own, precision=HIGH))
    house_grad = (dunit - unit_dirs * jnp.sum(unit_dirs * dunit, axis=-1, keepdims=True)) / lengths
    house_grad = house_grad.reshape(block_count, row_width)
    summed = jnp.zeros((w_query.shape[0], tok_rows), jnp.float32)
    for weight_mat, grad_mat in ((w_query, dq_out), (w_key, dk_out), (w_value, dv_out)):
        summed = summed + lax.dot_general(
            weight_mat, grad_mat, (((1,), (1,)), ((), ())), preferred_element_type=jnp.float32
        )
    share = lax.psum_scatter(
        summed.astype(jnp.bfloat16), "head", scatter_dimension=0, tiled=True
    ).astype(jnp.float32)
    return (share.T.astype(jnp.bfloat16), house_grad)


def solution(mesh):
    placed = (
        P("ctx", "head"),
        P("ctx", "head"),
        P("ctx", "head"),
        P("ctx", "head"),
        P("ctx", "head"),
        P("ctx", None),
        P("ctx", None),
        P(None, "head"),
        P(None, "head"),
        P(None, "head"),
    )
    return jax.shard_map(
        shards,
        mesh=mesh,
        in_specs=placed,
        out_specs=(P("ctx", "head"), P("ctx", "head")),
        check_vma=False,
    )
```

```python
import functools

import jax
import jax.numpy as jnp
from jax import lax
from jax.experimental import pallas as pl
from jax.experimental.pallas import tpu as pltpu
from jax.sharding import PartitionSpec as P

DH = 128
BLK = 128
MAXL = 2
CAP = 2
SIDE = 4
KINDS = 33

HIGH = lax.Precision.HIGHEST
MESH = pl.DeviceIdType.MESH
VMEM_BYTES = 60 * 1024 * 1024


def dot32(a, b, dims):
    return lax.dot_general(a, b, (dims, ((), ())), precision=HIGH, preferred_element_type=jnp.float32)


def dot16(a, b, dims):
    return lax.dot_general(a, b, (dims, ((), ())), preferred_element_type=jnp.float32)


NN = ((1,), (0,))
NT = ((1,), (1,))
TN = ((0,), (0,))


def place(me):
    return me // (2 * SIDE), lax.rem(me // 2, SIDE), lax.rem(me, 2)


def index_of(x, y, core):
    return (x * SIDE + y) * 2 + core


def turn(p, d):
    return lax.rem(p + d + SIDE, SIDE)


class Spread:
    def __init__(self, own, buf, send, recv, local_sem):
        self.own, self.buf, self.send, self.recv, self.local_sem = own, buf, send, recv, local_sem
        self.x, self.y, self.core = place(lax.axis_index("ctx"))
        self.rows = own.shape[0]
        self.started = []

    def view(self, path, phase, pos, quarter, core):
        half = self.rows // 2
        if quarter is None:
            rows = pl.ds(path * half, half)
        else:
            rows = pl.ds(path * half + quarter, half // 2)
        along_x = (path == 0) == (phase == 0)
        if phase == 0:
            if along_x:
                return self.buf.at[pos, self.y, core, rows]
            return self.buf.at[self.x, pos, core, rows]
        if along_x:
            return self.buf.at[pos, :, core, rows]
        return self.buf.at[:, pos, core, rows]

    def coord(self, path, phase):
        return self.x if (path == 0) == (phase == 0) else self.y

    def peer(self, path, phase, d):
        if (path == 0) == (phase == 0):
            return index_of(turn(self.x, d), self.y, self.core)
        return index_of(self.x, turn(self.y, d), self.core)

    def copy(self, src, dst, kind, device):
        return pltpu.make_async_remote_copy(
            src_ref=src,
            dst_ref=dst,
            send_sem=self.send.at[kind],
            recv_sem=self.recv.at[kind],
            device_id={"ctx": device},
            device_id_type=MESH,
        )

    def go(self, src, dst, kind, device):
        copy = self.copy(src, dst, kind, device)
        copy.start()
        self.started.append(copy)

    def partner(self):
        return index_of(self.x, self.y, 1 - self.core)

    def begin(self):
        mine = self.buf.at[self.x, self.y, self.core]
        local = pltpu.make_async_copy(self.own, mine, self.local_sem)
        local.start()
        half = self.rows // 2
        for path in range(2):
            rows = self.own.at[pl.ds(path * half, half)]
            dst = self.view(path, 0, self.coord(path, 0), None, self.core)
            for way, d in enumerate((1, -1)):
                self.go(rows, dst, path * 8 + way, self.peer(path, 0, d))
        self.go(self.own, mine, 32, self.partner())
        local.wait()

    def step(self, number):
        phase, late = number // 2, number % 2
        for path in range(2):
            at = self.coord(path, phase)
            for way, d in enumerate((1, -1)):
                kind = path * 8 + phase * 4 + late * 2 + way
                pos = turn(at, -d * (1 + late))
                quarter = way if late else None
                got = self.view(path, phase, pos, quarter, self.core)
                self.copy(got, got, kind, self.peer(path, phase, d)).wait_recv()
                if not late:
                    part = self.view(path, phase, pos, way, self.core)
                    self.go(part, part, kind + 2, self.peer(path, phase, d))
                self.go(got, got, 16 + kind, self.partner())
            if phase == 0 and late:
                full = self.view(path, 1, self.coord(path, 1), None, self.core)
                for way, d in enumerate((1, -1)):
                    self.go(full, full, path * 8 + 4 + way, self.peer(path, 1, d))

    def end(self):
        for kind in range(16):
            path, rest = divmod(kind, 8)
            phase, rest = divmod(rest, 4)
            late, way = divmod(rest, 2)
            d = (1, -1)[way]
            pos = turn(self.coord(path, phase), -d * (1 + late))
            got = self.view(path, phase, pos, way if late else None, 1 - self.core)
            self.copy(got, got, 16 + kind, self.partner()).wait_recv()
        theirs = self.buf.at[self.x, self.y, 1 - self.core]
        self.copy(theirs, theirs, 32, self.partner()).wait_recv()
        for copy in self.started:
            copy.wait_send()


def unit_rows(rows):
    square = rows * rows
    out = []
    for h in range(rows.shape[1] // DH):
        cols = slice(h * DH, (h + 1) * DH)
        length = jnp.sqrt(jnp.sum(square[:, cols], axis=1, keepdims=True) + 1e-06)
        out.append(rows[:, cols] / length)
    return out


def lower_inverse(gram, row, col):
    n = row.shape[0]

    def part_of(g, size):
        mask = (row // (2 * size) == col // (2 * size)) & (row // size > col // size)
        return jnp.where(mask, g, 0.0)

    eye2 = jnp.where(row == col, 2.0, 0.0)
    inv = [eye2 - 4.0 * part_of(g, 1) for g in gram]
    size = 2
    while size < n:
        inner = [dot32(part_of(g, size), i, NN) for g, i in zip(gram, inv)]
        inv = [i - dot32(i, w, NN) for i, w in zip(inv, inner)]
        size *= 2
    return inv


def split3(a):
    one = a.astype(jnp.bfloat16)
    rest = a - one.astype(jnp.float32)
    two = rest.astype(jnp.bfloat16)
    three = (rest - two.astype(jnp.float32)).astype(jnp.bfloat16)
    return one, two, three


def front_kernel(
    ids_ref, q_ref, k_ref, v_ref, house_ref,
    qrot_ref, krot_ref, rk_ref, rv_ref, prods_ref, units_ref, kmat_ref, solve_ref, hbuf,
    vbuf, kbuf, send_v, recv_v, send_k, recv_k, send_h, recv_h, local_sem,
):
    me = lax.axis_index("ctx")
    ctx = lax.axis_size("ctx")
    heads = q_ref.shape[2] // DH
    blocks = q_ref.shape[0]
    n = ctx * blocks

    barrier = pltpu.get_barrier_semaphore()
    for d in range(1, ctx):
        pl.semaphore_signal(
            barrier, inc=1, device_id={"ctx": lax.rem(me + d, ctx)}, device_id_type=MESH
        )
    pl.semaphore_wait(barrier, ctx - 1)

    small = []
    slot = hbuf.at[pl.ds(pl.multiple_of(me * 8, 8), 8)]
    for d in range(1, ctx):
        copy = pltpu.make_async_remote_copy(
            src_ref=house_ref,
            dst_ref=slot,
            send_sem=send_h.at[d],
            recv_sem=recv_h.at[d],
            device_id={"ctx": lax.rem(me + d, ctx)},
            device_id_type=MESH,
        )
        copy.start()
        small.append(copy)
    values = Spread(v_ref, vbuf, send_v, recv_v, local_sem.at[0])
    keys = Spread(krot_ref, kbuf, send_k, recv_k, local_sem.at[1])
    own = pltpu.make_async_copy(house_ref, slot, local_sem.at[2])
    own.start()
    values.begin()
    own.wait()
    for d in range(1, ctx):
        src = lax.rem(me - d + ctx, ctx)
        pltpu.make_async_remote_copy(
            src_ref=house_ref,
            dst_ref=hbuf.at[pl.ds(pl.multiple_of(src * 8, 8), 8)],
            send_sem=send_h.at[d],
            recv_sem=recv_h.at[d],
            device_id={"ctx": src},
            device_id_type=MESH,
        ).wait_recv()
    values.step(0)

    prow = lax.broadcasted_iota(jnp.int32, (n, 8 * ctx), 0)
    pcol = lax.broadcasted_iota(jnp.int32, (n, 8 * ctx), 1)
    pick = jnp.where(pcol == (prow // blocks) * 8 + prow % blocks, 1.0, 0.0)
    units = unit_rows(dot32(pick, hbuf[...], NN))
    row = lax.broadcasted_iota(jnp.int32, (n, n), 0)
    col = lax.broadcasted_iota(jnp.int32, (n, n), 1)
    gram = [dot32(u, u, NT) for u in units]
    solve = lower_inverse(gram, row, col)
    values.step(1)
    kmat = [dot32(s, u, NN) for s, u in zip(solve, units)]
    rows_n = lax.broadcasted_iota(jnp.int32, (n, DH), 0)
    eye = jnp.where(
        lax.broadcasted_iota(jnp.int32, (DH, DH), 0) == lax.broadcasted_iota(jnp.int32, (DH, DH), 1),
        1.0, 0.0,
    )
    for h in range(heads):
        cols = slice(h * DH, (h + 1) * DH)
        units_ref[:, cols] = units[h]
        kmat_ref[:, cols] = kmat[h]
        solve_ref[h] = solve[h]
        for b in range(blocks + 1):
            held = jnp.where(rows_n < me * blocks + b, units[h], 0.0)
            prod = eye - dot32(held, kmat[h], TN)
            prods_ref[b, :, cols] = prod
            if b > 0:
                pieces = split3(prod)
                for src, dst in ((k_ref, krot_ref), (q_ref, qrot_ref)):
                    tok = src[b - 1, :, cols]
                    acc = dot16(tok, pieces[2], NN) + dot16(tok, pieces[1], NN)
                    dst[b - 1, :, cols] = (acc + dot16(tok, pieces[0], NN)).astype(jnp.bfloat16)
    keys.begin()
    values.step(2)
    keys.step(0)
    values.step(3)
    keys.step(1)
    values.end()
    entries = rv_ref.shape[0]
    for e in range(entries):
        rv_ref[e] = vbuf[ids_ref[0, e], ids_ref[1, e], ids_ref[2, e], ids_ref[3, e]]
    keys.step(2)
    keys.step(3)
    keys.end()
    for e in range(entries):
        rk_ref[e] = kbuf[ids_ref[0, e], ids_ref[1, e], ids_ref[2, e], ids_ref[3, e]]
    for copy in small:
        copy.wait_send()


def front(ids, q, k, v, house8):
    ctx = lax.axis_size("ctx")
    blocks, _, width = q.shape
    heads = width // DH
    n = ctx * blocks
    entries = ids.shape[1]
    f32, bf16 = jnp.float32, jnp.bfloat16
    shape = jax.ShapeDtypeStruct
    vm = pl.BlockSpec(memory_space=pltpu.VMEM)
    return pl.pallas_call(
        front_kernel,
        out_shape=(
            shape(q.shape, bf16), shape(q.shape, bf16),
            shape((entries, BLK, width), bf16), shape((entries, BLK, width), bf16),
            shape((blocks + 1, DH, width), f32), shape((n, width), f32),
            shape((n, width), f32), shape((heads, n, n), f32), shape((8 * ctx, width), f32),
        ),
        in_specs=[pl.BlockSpec(memory_space=pltpu.SMEM), vm, vm, vm, vm],
        out_specs=(vm,) * 9,
        scratch_shapes=[
            pltpu.VMEM((SIDE, SIDE, 2) + q.shape, bf16),
            pltpu.VMEM((SIDE, SIDE, 2) + q.shape, bf16),
            pltpu.SemaphoreType.DMA((KINDS,)), pltpu.SemaphoreType.DMA((KINDS,)),
            pltpu.SemaphoreType.DMA((KINDS,)), pltpu.SemaphoreType.DMA((KINDS,)),
            pltpu.SemaphoreType.DMA((ctx,)), pltpu.SemaphoreType.DMA((ctx,)),
            pltpu.SemaphoreType.DMA((3,)),
        ],
        compiler_params=pltpu.CompilerParams(
            collective_id=0, has_side_effects=True, vmem_limit_bytes=VMEM_BYTES
        ),
        name="front",
    )(ids, q, k, v, house8)


def attend_kernel(
    slot_ref, q_ref, k_ref, v_ref, g_ref, rk_ref, rv_ref, dq_ref, dk_ref, dv_ref, part_ref
):
    part_ref[...] = jnp.zeros_like(part_ref)
    heads = q_ref.shape[1] // DH
    blocks = q_ref.shape[0] // BLK
    scaling = DH ** (-0.5)
    diag = lax.broadcasted_iota(jnp.int32, (BLK, BLK), 0) >= lax.broadcasted_iota(
        jnp.int32, (BLK, BLK), 1
    )
    for h in range(heads):
        cols = slice(h * DH, (h + 1) * DH)
        for b in range(blocks):
            rows = slice(b * BLK, (b + 1) * BLK)
            q, g = q_ref[rows, cols], g_ref[rows, cols]
            rem = range(b * MAXL, (b + 1) * MAXL)
            ks = [k_ref[j * BLK : (j + 1) * BLK, cols] for j in range(b + 1)]
            vs = [v_ref[j * BLK : (j + 1) * BLK, cols] for j in range(b + 1)]
            ks += [rk_ref[e, :, cols] for e in rem]
            vs += [rv_ref[e, :, cols] for e in rem]
            kcat, vcat = jnp.concatenate(ks, axis=0), jnp.concatenate(vs, axis=0)
            s = dot16(q, kcat, NT) * scaling
            parts = [s[:, j * BLK : (j + 1) * BLK] for j in range(len(ks))]
            parts[b] = jnp.where(diag, parts[b], -jnp.inf)
            s = jnp.concatenate(parts, axis=1)
            top = jnp.max(s, axis=1, keepdims=True)
            ex = jnp.exp(s - top)
            lse = top + jnp.log(jnp.sum(ex, axis=1, keepdims=True))
            p = jnp.exp(s - lse)
            pb = p.astype(jnp.bfloat16)
            att = dot16(pb, vcat, NN)
            delta = jnp.sum(g.astype(jnp.float32) * att, axis=1, keepdims=True)
            dp = dot16(g, vcat, NT)
            ds = (p * (dp - delta)).astype(jnp.bfloat16)
            dq_ref[rows, cols] = scaling * dot16(ds, kcat, NN)
            dk = scaling * dot16(ds, q, TN)
            dv = dot16(pb, g, TN)
            for j in range(b + 1):
                to = slice(j * BLK, (j + 1) * BLK)
                if j == b:
                    dk_ref[to, cols] = dk[to]
                    dv_ref[to, cols] = dv[to]
                else:
                    dk_ref[to, cols] += dk[to]
                    dv_ref[to, cols] += dv[to]
            for i, e in enumerate(rem):
                at = slice((b + 1 + i) * BLK, (b + 2 + i) * BLK)
                part_ref[slot_ref[e], 0, :, cols] = dk[at].astype(jnp.bfloat16)
                part_ref[slot_ref[e], 1, :, cols] = dv[at].astype(jnp.bfloat16)


def attend(slots, slot_count, q, k, v, g, rk, rv):
    tok, width = q.shape
    shape = jax.ShapeDtypeStruct
    vm = pl.BlockSpec(memory_space=pltpu.VMEM)
    full = shape((tok, width), jnp.float32)
    return pl.pallas_call(
        attend_kernel,
        out_shape=(full, full, full, shape((slot_count, 2, BLK, width), jnp.bfloat16)),
        in_specs=[pl.BlockSpec(memory_space=pltpu.SMEM)] + [vm] * 6,
        out_specs=(vm,) * 4,
        compiler_params=pltpu.CompilerParams(vmem_limit_bytes=VMEM_BYTES),
        name="attend",
    )(slots, q, k, v, g, rk, rv)


def owner_ranks(owner_lists, before):
    same_owner = owner_lists[..., :, None] == owner_lists[..., None, :]
    return jnp.sum((same_owner & before).astype(jnp.int32), axis=-1)


def reflect_apply(unit_dirs, matrices):
    projected = jnp.einsum("hn,hnk->hk", unit_dirs, matrices, precision=HIGH)
    return matrices - 2.0 * unit_dirs[:, :, None] * projected[:, None, :]


def shards(
    query_rows, key_rows, value_rows, grad_out, house_dirs, owners, offsets, w_query, w_key, w_value
):
    tok_rows, row_width = query_rows.shape
    head_count = row_width // DH
    block_count = tok_rows // BLK
    entries = block_count * MAXL
    ctx_count = lax.axis_size("ctx")
    all_blocks = ctx_count * block_count
    ctx_count = lax.axis_size("ctx")
    first = lax.axis_index("ctx") * block_count
    own_flat, offset_flat = owners.reshape(entries), offsets.reshape(entries)
    entry_order = jnp.arange(entries)
    before = entry_order[None, :] < entry_order[:, None]
    slot_ids = own_flat * CAP + owner_ranks(own_flat, before)
    where = jnp.stack([own_flat // 8, own_flat // 2 % 4, own_flat % 2, offset_flat])
    listed = jnp.stack([own_flat, offset_flat]).astype(jnp.float32).reshape(1, 2 * entries)
    house8 = jnp.concatenate([house_dirs, jnp.pad(listed, ((0, 3), (0, row_width - 2 * entries)))])

    def blocked(rows):
        return rows.reshape(block_count, BLK, row_width)

    query_rot, key_rot, remote_keys, remote_values, prods, units, kmat, solve, small = front(
        where, blocked(query_rows), blocked(key_rows), blocked(value_rows), house8
    )
    dq_rot, dk_local, dv_local, parts = attend(
        slot_ids, CAP * ctx_count, query_rot.reshape(tok_rows, row_width),
        key_rot.reshape(tok_rows, row_width), value_rows, grad_out, remote_keys, remote_values
    )
    lists = small.reshape(ctx_count, 8, row_width)[:, block_count, : 2 * entries].astype(jnp.int32)
    all_owner, all_offset = lists[:, :entries], lists[:, entries:]
    all_rank = owner_ranks(all_owner, before)
    matched = (all_owner[:, :, None] == lax.axis_index("ctx")) & (
        all_rank[:, :, None] == jnp.arange(CAP)[None, None, :]
    )
    table = jnp.any(
        matched[:, :, None, :]
        & (all_offset[:, :, None, None] == jnp.arange(block_count)[None, None, :, None]),
        axis=1,
    )
    table = table.transpose(1, 0, 2).reshape(block_count, ctx_count * CAP).astype(jnp.bfloat16)
    ids = jnp.arange(all_blocks)
    below = ids < first
    prods = prods.reshape(block_count + 1, DH, head_count, DH).transpose(0, 2, 1, 3)
    previous, cumulative = prods[:-1], prods[1:]
    units_all = units.reshape(all_blocks, head_count, DH).transpose(1, 0, 2)
    k_all = kmat.reshape(all_blocks, head_count, DH).transpose(1, 0, 2)
    house_heads = house_dirs.reshape(block_count, head_count, DH)
    lengths = jnp.sqrt(jnp.sum(house_heads * house_heads, axis=-1, keepdims=True) + 1e-06)
    unit_dirs = house_heads / lengths
    query_f32 = query_rows.astype(jnp.float32).reshape(block_count, BLK, head_count, DH)
    key_f32 = key_rows.astype(jnp.float32).reshape(block_count, BLK, head_count, DH)
    back = lax.all_to_all(parts, "ctx", split_axis=0, concat_axis=0, tiled=True)
    back = jnp.einsum("bs,skrw->kbrw", table, back, preferred_element_type=jnp.float32)
    dk_rot = (blocked(dk_local) + back[0]).reshape(block_count, BLK, head_count, DH)
    dv_out = (blocked(dv_local) + back[1]).astype(jnp.bfloat16).reshape(tok_rows, row_width)
    dq_rot = dq_rot.reshape(block_count, BLK, head_count, DH)
    dq_out = (
        jnp.einsum("bthm,bhnm->bthn", dq_rot, cumulative, precision=HIGH)
        .astype(jnp.bfloat16)
        .reshape(tok_rows, row_width)
    )
    dk_out = (
        jnp.einsum("bthm,bhnm->bthn", dk_rot, cumulative, precision=HIGH)
        .astype(jnp.bfloat16)
        .reshape(tok_rows, row_width)
    )
    dcum = jnp.einsum("bthn,bthm->bhnm", query_f32, dq_rot, precision=HIGH)
    dcum = dcum + jnp.einsum("bthn,bthm->bhnm", key_f32, dk_rot, precision=HIGH)

    carry = jnp.zeros((head_count, DH, DH), jnp.float32)
    adjoints = [None] * block_count
    for block in range(block_count - 1, -1, -1):
        adjoints[block] = dcum[block] + carry
        carry = reflect_apply(unit_dirs[block], adjoints[block])
    held = below[None, :, None].astype(jnp.float32)
    units_below = units_all * held
    k_below = k_all * held
    through = jnp.einsum("hin,hnm->him", units_below, carry, precision=HIGH)
    to_z = 0.5 * jnp.einsum("hib,him->hbm", solve, through, precision=HIGH)
    crossed = jnp.einsum("hbm,him->hbi", k_below, through, precision=HIGH)
    crossed = jnp.einsum("hbj,hji->hbi", crossed, solve, precision=HIGH)
    crossed = jnp.where(ids[:, None] < ids[None, :], crossed, 0.0)
    to_y = jnp.einsum("hbm,hnm->hbn", k_below, carry, precision=HIGH) - jnp.einsum(
        "hbi,hin->hbn", crossed, units_all, precision=HIGH
    )
    sent = jnp.stack([to_y, to_z], axis=0).transpose(2, 0, 1, 3).reshape(all_blocks, 4 * DH)
    came = lax.all_to_all(
        sent.reshape(ctx_count, block_count, 4 * DH), "ctx", split_axis=0, concat_axis=0, tiled=True
    )
    came = jnp.sum(came, axis=0).reshape(block_count, 2, head_count, DH)
    adjoint = jnp.stack(adjoints)
    k_own = lax.dynamic_slice_in_dim(k_all, first, block_count, axis=1)
    y_own = came[:, 0] + jnp.einsum("bhnm,hbm->bhn", adjoint, k_own, precision=HIGH)
    z_own = came[:, 1] + jnp.einsum("bhnm,bhn->bhm", adjoint, unit_dirs, precision=HIGH)
    dunit = -2.0 * (0.5 * y_own + jnp.einsum("bhnm,bhm->bhn", previous, z_own, precision=HIGH))
    house_grad = (dunit - unit_dirs * jnp.sum(unit_dirs * dunit, axis=-1, keepdims=True)) / lengths
    house_grad = house_grad.reshape(block_count, row_width)
    summed = jnp.zeros((w_query.shape[0], tok_rows), jnp.float32)
    for weight_mat, grad_mat in ((w_query, dq_out), (w_key, dk_out), (w_value, dv_out)):
        summed = summed + lax.dot_general(
            weight_mat, grad_mat, (((1,), (1,)), ((), ())), preferred_element_type=jnp.float32
        )
    share = lax.psum_scatter(
        summed.astype(jnp.bfloat16), "head", scatter_dimension=0, tiled=True
    ).astype(jnp.float32)
    return (share.T.astype(jnp.bfloat16), house_grad)


def solution(mesh):
    placed = (
        P("ctx", "head"),
        P("ctx", "head"),
        P("ctx", "head"),
        P("ctx", "head"),
        P("ctx", "head"),
        P("ctx", None),
        P("ctx", None),
        P(None, "head"),
        P(None, "head"),
        P(None, "head"),
    )
    return jax.shard_map(
        shards,
        mesh=mesh,
        in_specs=placed,
        out_specs=(P("ctx", "head"), P("ctx", "head")),
        check_vma=False,
    )
```

```python
import jax
import jax.numpy as jnp
from jax import lax
from jax.experimental import pallas as pl
from jax.experimental.pallas import tpu as pltpu
from jax.sharding import PartitionSpec as P

DH = 128
BLK = 128
MAXL = 2
SIDE = 4
KINDS = 33

HIGH = lax.Precision.HIGHEST
MESH = pl.DeviceIdType.MESH
VMEM_BYTES = 60 * 1024 * 1024


def dot32(a, b, dims):
    return lax.dot_general(a, b, (dims, ((), ())), precision=HIGH, preferred_element_type=jnp.float32)


def dot16(a, b, dims):
    return lax.dot_general(a, b, (dims, ((), ())), preferred_element_type=jnp.float32)


NN = ((1,), (0,))
NT = ((1,), (1,))
TN = ((0,), (0,))


def place(me):
    return me // (2 * SIDE), lax.rem(me // 2, SIDE), lax.rem(me, 2)


def index_of(x, y, core):
    return (x * SIDE + y) * 2 + core


def turn(p, d):
    return lax.rem(p + d + SIDE, SIDE)


class Spread:
    def __init__(self, own, buf, send, recv, local_sem):
        self.own, self.buf, self.send, self.recv, self.local_sem = own, buf, send, recv, local_sem
        self.x, self.y, self.core = place(lax.axis_index("ctx"))
        self.rows = own.shape[0]
        self.started = []

    def view(self, path, phase, pos, quarter, core):
        half = self.rows // 2
        if quarter is None:
            rows = pl.ds(path * half, half)
        else:
            rows = pl.ds(path * half + quarter, half // 2)
        along_x = (path == 0) == (phase == 0)
        if phase == 0:
            if along_x:
                return self.buf.at[pos, self.y, core, rows]
            return self.buf.at[self.x, pos, core, rows]
        if along_x:
            return self.buf.at[pos, :, core, rows]
        return self.buf.at[:, pos, core, rows]

    def coord(self, path, phase):
        return self.x if (path == 0) == (phase == 0) else self.y

    def peer(self, path, phase, d):
        if (path == 0) == (phase == 0):
            return index_of(turn(self.x, d), self.y, self.core)
        return index_of(self.x, turn(self.y, d), self.core)

    def copy(self, src, dst, kind, device):
        return pltpu.make_async_remote_copy(
            src_ref=src,
            dst_ref=dst,
            send_sem=self.send.at[kind],
            recv_sem=self.recv.at[kind],
            device_id={"ctx": device},
            device_id_type=MESH,
        )

    def go(self, src, dst, kind, device):
        copy = self.copy(src, dst, kind, device)
        copy.start()
        self.started.append(copy)

    def partner(self):
        return index_of(self.x, self.y, 1 - self.core)

    def begin(self):
        mine = self.buf.at[self.x, self.y, self.core]
        local = pltpu.make_async_copy(self.own, mine, self.local_sem)
        local.start()
        half = self.rows // 2
        for path in range(2):
            rows = self.own.at[pl.ds(path * half, half)]
            dst = self.view(path, 0, self.coord(path, 0), None, self.core)
            for way, d in enumerate((1, -1)):
                self.go(rows, dst, path * 8 + way, self.peer(path, 0, d))
        self.go(self.own, mine, 32, self.partner())
        local.wait()

    def step(self, number):
        phase, late = number // 2, number % 2
        for path in range(2):
            at = self.coord(path, phase)
            for way, d in enumerate((1, -1)):
                kind = path * 8 + phase * 4 + late * 2 + way
                pos = turn(at, -d * (1 + late))
                quarter = way if late else None
                got = self.view(path, phase, pos, quarter, self.core)
                self.copy(got, got, kind, self.peer(path, phase, d)).wait_recv()
                if not late:
                    part = self.view(path, phase, pos, way, self.core)
                    self.go(part, part, kind + 2, self.peer(path, phase, d))
                self.go(got, got, 16 + kind, self.partner())
            if phase == 0 and late:
                full = self.view(path, 1, self.coord(path, 1), None, self.core)
                for way, d in enumerate((1, -1)):
                    self.go(full, full, path * 8 + 4 + way, self.peer(path, 1, d))

    def end(self):
        for kind in range(16):
            path, rest = divmod(kind, 8)
            phase, rest = divmod(rest, 4)
            late, way = divmod(rest, 2)
            d = (1, -1)[way]
            pos = turn(self.coord(path, phase), -d * (1 + late))
            got = self.view(path, phase, pos, way if late else None, 1 - self.core)
            self.copy(got, got, 16 + kind, self.partner()).wait_recv()
        theirs = self.buf.at[self.x, self.y, 1 - self.core]
        self.copy(theirs, theirs, 32, self.partner()).wait_recv()
        for copy in self.started:
            copy.wait_send()


def unit_rows(rows):
    square = rows * rows
    out = []
    for h in range(rows.shape[1] // DH):
        cols = slice(h * DH, (h + 1) * DH)
        length = jnp.sqrt(jnp.sum(square[:, cols], axis=1, keepdims=True) + 1e-06)
        out.append(rows[:, cols] / length)
    return out


def lower_inverse(gram, row, col):
    n = row.shape[0]

    def part_of(g, size):
        mask = (row // (2 * size) == col // (2 * size)) & (row // size > col // size)
        return jnp.where(mask, g, 0.0)

    eye2 = jnp.where(row == col, 2.0, 0.0)
    inv = [eye2 - 4.0 * part_of(g, 1) for g in gram]
    size = 2
    while size < n:
        inner = [dot32(part_of(g, size), i, NN) for g, i in zip(gram, inv)]
        inv = [i - dot32(i, w, NN) for i, w in zip(inv, inner)]
        size *= 2
    return inv


def split3(a):
    one = a.astype(jnp.bfloat16)
    rest = a - one.astype(jnp.float32)
    two = rest.astype(jnp.bfloat16)
    three = (rest - two.astype(jnp.float32)).astype(jnp.bfloat16)
    return one, two, three


def front_kernel(
    ids_ref, q_ref, k_ref, v_ref, house_ref,
    qrot_ref, krot_ref, rk_ref, rv_ref, prods_ref, units_ref, kmat_ref, solve_ref, hbuf,
    vbuf, kbuf, send_v, recv_v, send_k, recv_k, send_h, recv_h, local_sem,
):
    me = lax.axis_index("ctx")
    ctx = lax.axis_size("ctx")
    heads = q_ref.shape[2] // DH
    blocks = q_ref.shape[0]
    n = ctx * blocks

    barrier = pltpu.get_barrier_semaphore()
    for d in range(1, ctx):
        pl.semaphore_signal(
            barrier, inc=1, device_id={"ctx": lax.rem(me + d, ctx)}, device_id_type=MESH
        )
    pl.semaphore_wait(barrier, ctx - 1)

    small = []
    slot = hbuf.at[pl.ds(pl.multiple_of(me * 8, 8), 8)]
    for d in range(1, ctx):
        copy = pltpu.make_async_remote_copy(
            src_ref=house_ref,
            dst_ref=slot,
            send_sem=send_h.at[d],
            recv_sem=recv_h.at[d],
            device_id={"ctx": lax.rem(me + d, ctx)},
            device_id_type=MESH,
        )
        copy.start()
        small.append(copy)
    values = Spread(v_ref, vbuf, send_v, recv_v, local_sem.at[0])
    keys = Spread(krot_ref, kbuf, send_k, recv_k, local_sem.at[1])
    own = pltpu.make_async_copy(house_ref, slot, local_sem.at[2])
    own.start()
    values.begin()
    own.wait()
    for d in range(1, ctx):
        src = lax.rem(me - d + ctx, ctx)
        pltpu.make_async_remote_copy(
            src_ref=house_ref,
            dst_ref=hbuf.at[pl.ds(pl.multiple_of(src * 8, 8), 8)],
            send_sem=send_h.at[d],
            recv_sem=recv_h.at[d],
            device_id={"ctx": src},
            device_id_type=MESH,
        ).wait_recv()
    values.step(0)

    prow = lax.broadcasted_iota(jnp.int32, (n, 8 * ctx), 0)
    pcol = lax.broadcasted_iota(jnp.int32, (n, 8 * ctx), 1)
    pick = jnp.where(pcol == (prow // blocks) * 8 + prow % blocks, 1.0, 0.0)
    units = unit_rows(dot32(pick, hbuf[...], NN))
    row = lax.broadcasted_iota(jnp.int32, (n, n), 0)
    col = lax.broadcasted_iota(jnp.int32, (n, n), 1)
    gram = [dot32(u, u, NT) for u in units]
    solve = lower_inverse(gram, row, col)
    values.step(1)
    kmat = [dot32(s, u, NN) for s, u in zip(solve, units)]
    rows_n = lax.broadcasted_iota(jnp.int32, (n, DH), 0)
    eye = jnp.where(
        lax.broadcasted_iota(jnp.int32, (DH, DH), 0) == lax.broadcasted_iota(jnp.int32, (DH, DH), 1),
        1.0, 0.0,
    )
    for h in range(heads):
        cols = slice(h * DH, (h + 1) * DH)
        units_ref[:, cols] = units[h]
        kmat_ref[:, cols] = kmat[h]
        solve_ref[h] = solve[h]
        for b in range(blocks + 1):
            held = jnp.where(rows_n < me * blocks + b, units[h], 0.0)
            prod = eye - dot32(held, kmat[h], TN)
            prods_ref[b, :, cols] = prod
            if b > 0:
                pieces = split3(prod)
                for src, dst in ((k_ref, krot_ref), (q_ref, qrot_ref)):
                    tok = src[b - 1, :, cols]
                    acc = dot16(tok, pieces[2], NN) + dot16(tok, pieces[1], NN)
                    dst[b - 1, :, cols] = (acc + dot16(tok, pieces[0], NN)).astype(jnp.bfloat16)
    keys.begin()
    values.step(2)
    keys.step(0)
    values.step(3)
    keys.step(1)
    values.end()
    entries = rv_ref.shape[0]
    for e in range(entries):
        rv_ref[e] = vbuf[ids_ref[0, e], ids_ref[1, e], ids_ref[2, e], ids_ref[3, e]]
    keys.step(2)
    keys.step(3)
    keys.end()
    for e in range(entries):
        rk_ref[e] = kbuf[ids_ref[0, e], ids_ref[1, e], ids_ref[2, e], ids_ref[3, e]]
    for copy in small:
        copy.wait_send()


def front(ids, q, k, v, house8):
    ctx = lax.axis_size("ctx")
    blocks, _, width = q.shape
    heads = width // DH
    n = ctx * blocks
    entries = ids.shape[1]
    f32, bf16 = jnp.float32, jnp.bfloat16
    shape = jax.ShapeDtypeStruct
    vm = pl.BlockSpec(memory_space=pltpu.VMEM)
    return pl.pallas_call(
        front_kernel,
        out_shape=(
            shape(q.shape, bf16), shape(q.shape, bf16),
            shape((entries, BLK, width), bf16), shape((entries, BLK, width), bf16),
            shape((blocks + 1, DH, width), f32), shape((n, width), f32),
            shape((n, width), f32), shape((heads, n, n), f32), shape((8 * ctx, width), f32),
        ),
        in_specs=[pl.BlockSpec(memory_space=pltpu.SMEM), vm, vm, vm, vm],
        out_specs=(vm,) * 9,
        scratch_shapes=[
            pltpu.VMEM((SIDE, SIDE, 2) + q.shape, bf16),
            pltpu.VMEM((SIDE, SIDE, 2) + q.shape, bf16),
            pltpu.SemaphoreType.DMA((KINDS,)), pltpu.SemaphoreType.DMA((KINDS,)),
            pltpu.SemaphoreType.DMA((KINDS,)), pltpu.SemaphoreType.DMA((KINDS,)),
            pltpu.SemaphoreType.DMA((ctx,)), pltpu.SemaphoreType.DMA((ctx,)),
            pltpu.SemaphoreType.DMA((3,)),
        ],
        compiler_params=pltpu.CompilerParams(
            collective_id=0, has_side_effects=True, vmem_limit_bytes=VMEM_BYTES
        ),
        name="front",
    )(ids, q, k, v, house8)


def attend_kernel(
    q_ref, k_ref, v_ref, g_ref, rk_ref, rv_ref, dq_ref, dk_ref, dv_ref, part_ref
):
    none = part_ref.shape[0] - 1
    part_ref[none] = jnp.zeros(part_ref.shape[1:], jnp.bfloat16)
    heads = q_ref.shape[1] // DH
    blocks = q_ref.shape[0] // BLK
    scaling = DH ** (-0.5)
    diag = lax.broadcasted_iota(jnp.int32, (BLK, BLK), 0) >= lax.broadcasted_iota(
        jnp.int32, (BLK, BLK), 1
    )
    for h in range(heads):
        cols = slice(h * DH, (h + 1) * DH)
        for b in range(blocks):
            rows = slice(b * BLK, (b + 1) * BLK)
            q, g = q_ref[rows, cols], g_ref[rows, cols]
            rem = range(b * MAXL, (b + 1) * MAXL)
            ks = [k_ref[j * BLK : (j + 1) * BLK, cols] for j in range(b + 1)]
            vs = [v_ref[j * BLK : (j + 1) * BLK, cols] for j in range(b + 1)]
            ks += [rk_ref[e, :, cols] for e in rem]
            vs += [rv_ref[e, :, cols] for e in rem]
            kcat, vcat = jnp.concatenate(ks, axis=0), jnp.concatenate(vs, axis=0)
            s = dot16(q, kcat, NT) * scaling
            parts = [s[:, j * BLK : (j + 1) * BLK] for j in range(len(ks))]
            parts[b] = jnp.where(diag, parts[b], -jnp.inf)
            s = jnp.concatenate(parts, axis=1)
            top = jnp.max(s, axis=1, keepdims=True)
            ex = jnp.exp(s - top)
            lse = top + jnp.log(jnp.sum(ex, axis=1, keepdims=True))
            p = jnp.exp(s - lse)
            pb = p.astype(jnp.bfloat16)
            att = dot16(pb, vcat, NN)
            delta = jnp.sum(g.astype(jnp.float32) * att, axis=1, keepdims=True)
            dp = dot16(g, vcat, NT)
            ds = (p * (dp - delta)).astype(jnp.bfloat16)
            dq_ref[rows, cols] = scaling * dot16(ds, kcat, NN)
            dk = scaling * dot16(ds, q, TN)
            dv = dot16(pb, g, TN)
            for j in range(b + 1):
                to = slice(j * BLK, (j + 1) * BLK)
                if j == b:
                    dk_ref[to, cols] = dk[to]
                    dv_ref[to, cols] = dv[to]
                else:
                    dk_ref[to, cols] += dk[to]
                    dv_ref[to, cols] += dv[to]
            for i, e in enumerate(rem):
                at = slice((b + 1 + i) * BLK, (b + 2 + i) * BLK)
                part_ref[e, 0, :, cols] = dk[at].astype(jnp.bfloat16)
                part_ref[e, 1, :, cols] = dv[at].astype(jnp.bfloat16)


def attend(q, k, v, g, rk, rv):
    tok, width = q.shape
    shape = jax.ShapeDtypeStruct
    vm = pl.BlockSpec(memory_space=pltpu.VMEM)
    full = shape((tok, width), jnp.float32)
    return pl.pallas_call(
        attend_kernel,
        out_shape=(full, full, full, shape((rk.shape[0] + 1, 2, BLK, width), jnp.bfloat16)),
        in_specs=[vm] * 6,
        out_specs=(vm,) * 4,
        compiler_params=pltpu.CompilerParams(vmem_limit_bytes=VMEM_BYTES),
        name="attend",
    )(q, k, v, g, rk, rv)


def collect_kernel(
    table_ref, part_ref, out_ref,
    theirs, acc, near1, full1, near2, full2, send, recv, pair_send, pair_recv,
):
    x, y, core = place(lax.axis_index("ctx"))
    partner = index_of(x, y, 1 - core)

    def peer(along_x, d):
        if along_x:
            return index_of(turn(x, d), y, core)
        return index_of(x, turn(y, d), core)

    barrier = pltpu.get_barrier_semaphore()
    for device in (partner, peer(True, 1), peer(True, -1), peer(False, 1), peer(False, -1)):
        pl.semaphore_signal(barrier, inc=1, device_id={"ctx": device}, device_id_type=MESH)
    pl.semaphore_wait(barrier, 5)

    started = []

    def copy_of(src, dst, send_sem, recv_sem, device):
        return pltpu.make_async_remote_copy(
            src_ref=src,
            dst_ref=dst,
            send_sem=send_sem,
            recv_sem=recv_sem,
            device_id={"ctx": device},
            device_id_type=MESH,
        )

    pair = copy_of(part_ref, theirs, pair_send.at[0], pair_recv.at[0], partner)
    pair.start()
    pair.wait_recv()
    started.append(pair)

    def chunk(kv, path, stage, pos, first, count):
        rows = pl.ds(path * 2 + first, count)
        if stage == 0:
            return acc.at[kv, :, pos, rows] if path == 0 else acc.at[kv, pos, :, rows]
        return acc.at[kv, pos, y, rows] if path == 0 else acc.at[kv, x, pos, rows]

    def coord(path, stage):
        along_x = (path == 0) == (stage == 1)
        return along_x, (x if along_x else y)

    def landing(kv, path, stage, step, way):
        buf = ((near1, full1), (near2, full2))[stage][step]
        return buf.at[kv, path, way]

    def kind_of(kv, path, stage, step, way):
        return (((kv * 2 + path) * 2 + stage) * 2 + step) * 2 + way

    def send_on(kv, path, stage, step):
        along_x, at = coord(path, stage)
        for way, d in enumerate((1, -1)):
            kind = kind_of(kv, path, stage, step, way)
            if step == 0:
                src = chunk(kv, path, stage, turn(at, 2), way, 1)
            else:
                src = chunk(kv, path, stage, turn(at, d), 0, 2)
            copy = copy_of(
                src, landing(kv, path, stage, step, way), send.at[kind], recv.at[kind],
                peer(along_x, d),
            )
            copy.start()
            started.append(copy)

    def take(kv, path, stage, step):
        along_x, at = coord(path, stage)
        for way, d in enumerate((1, -1)):
            kind = kind_of(kv, path, stage, step, way)
            got = landing(kv, path, stage, step, way)
            copy_of(got, got, send.at[kind], recv.at[kind], peer(along_x, d)).wait_recv()
            if stage == 1 and step == 1:
                continue
            pos = turn(at, d) if step == 0 else at
            first, count = (way, 1) if step == 0 else (0, 2)
            for b in range(count):
                row = path * 2 + first + b
                if stage == 1:
                    where = (kv, pos, y, row) if path == 0 else (kv, x, pos, row)
                    acc[where] = acc[where] + got[b]
                    continue
                for i in range(SIDE):
                    where = (kv, i, pos, row) if path == 0 else (kv, pos, i, row)
                    acc[where] = acc[where] + got[i, b]

    both = [(kv, path) for kv in range(2) for path in range(2)]
    for kv in range(2):

        def build(i, carry, kv=kv):
            where = (kv, i // (4 * SIDE), i // 4 % SIDE, i % 4)
            mine = part_ref[table_ref[0, i], kv] + part_ref[table_ref[1, i], kv]
            other = theirs[table_ref[2, i], kv] + theirs[table_ref[3, i], kv]
            acc[where] = mine + other
            return carry

        lax.fori_loop(0, 4 * SIDE * SIDE, build, 0)
        for path in range(2):
            send_on(kv, path, 0, 0)
    for kv, path in both:
        take(kv, path, 0, 0)
        send_on(kv, path, 0, 1)
    for kv, path in both:
        take(kv, path, 0, 1)
        send_on(kv, path, 1, 0)
    for kv, path in both:
        take(kv, path, 1, 0)
        send_on(kv, path, 1, 1)
    for kv, path in both:
        take(kv, path, 1, 1)
        for b in range(2):
            row = path * 2 + b
            total = acc[kv, x, y, row].astype(jnp.float32)
            for way in range(2):
                total = total + full2[kv, path, way, b].astype(jnp.float32)
            out_ref[kv, row] = total
    for copy in started:
        copy.wait_send()


def collect(table, parts):
    _, _, rows, width = parts.shape
    bf16 = jnp.bfloat16
    vm = pl.BlockSpec(memory_space=pltpu.VMEM)
    return pl.pallas_call(
        collect_kernel,
        out_shape=jax.ShapeDtypeStruct((2, 4, rows, width), jnp.float32),
        in_specs=[pl.BlockSpec(memory_space=pltpu.SMEM), vm],
        out_specs=vm,
        scratch_shapes=[
            pltpu.VMEM(parts.shape, bf16),
            pltpu.VMEM((2, SIDE, SIDE, 4, rows, width), bf16),
            pltpu.VMEM((2, 2, 2, SIDE, 1, rows, width), bf16),
            pltpu.VMEM((2, 2, 2, SIDE, 2, rows, width), bf16),
            pltpu.VMEM((2, 2, 2, 1, rows, width), bf16),
            pltpu.VMEM((2, 2, 2, 2, rows, width), bf16),
            pltpu.SemaphoreType.DMA((32,)), pltpu.SemaphoreType.DMA((32,)),
            pltpu.SemaphoreType.DMA((1,)), pltpu.SemaphoreType.DMA((1,)),
        ],
        compiler_params=pltpu.CompilerParams(
            collective_id=1, has_side_effects=True, vmem_limit_bytes=VMEM_BYTES
        ),
        name="collect",
    )(table, parts)


def reflect_apply(unit_dirs, matrices):
    projected = jnp.einsum("hn,hnk->hk", unit_dirs, matrices, precision=HIGH)
    return matrices - 2.0 * unit_dirs[:, :, None] * projected[:, None, :]


def shards(
    query_rows, key_rows, value_rows, grad_out, house_dirs, owners, offsets, w_query, w_key, w_value
):
    tok_rows, row_width = query_rows.shape
    head_count = row_width // DH
    block_count = tok_rows // BLK
    entries = block_count * MAXL
    ctx_count = lax.axis_size("ctx")
    all_blocks = ctx_count * block_count
    ctx_count = lax.axis_size("ctx")
    first = lax.axis_index("ctx") * block_count
    own_flat, offset_flat = owners.reshape(entries), offsets.reshape(entries)
    where = jnp.stack([own_flat // 8, own_flat // 2 % 4, own_flat % 2, offset_flat])
    listed = jnp.stack([own_flat, offset_flat]).astype(jnp.float32).reshape(1, 2 * entries)
    house8 = jnp.concatenate([house_dirs, jnp.pad(listed, ((0, 3), (0, row_width - 2 * entries)))])

    def blocked(rows):
        return rows.reshape(block_count, BLK, row_width)

    query_rot, key_rot, remote_keys, remote_values, prods, units, kmat, solve, small = front(
        where, blocked(query_rows), blocked(key_rows), blocked(value_rows), house8
    )
    dq_rot, dk_local, dv_local, parts = attend(
        query_rot.reshape(tok_rows, row_width),
        key_rot.reshape(tok_rows, row_width), value_rows, grad_out, remote_keys, remote_values
    )
    me = lax.axis_index("ctx")
    lists = small.reshape(ctx_count, 8, row_width)[:, block_count, : 2 * entries].astype(jnp.int32)
    theirs = lax.dynamic_index_in_dim(lists, me + 1 - 2 * (me % 2), keepdims=False)
    spot = jnp.arange(ctx_count // 2 * block_count)
    spot_owner, spot_offset = spot // block_count * 2 + me % 2, spot % block_count
    entry_order = jnp.arange(entries)

    def listed_at(owner, offset):
        hit = (owner[None, :] == spot_owner[:, None]) & (offset[None, :] == spot_offset[:, None])
        low = jnp.min(jnp.where(hit, entry_order, entries), axis=1)
        high = jnp.max(jnp.where(hit, entry_order, -1), axis=1)
        return [low, jnp.where(high > low, high, entries)]

    table = jnp.stack(
        listed_at(own_flat, offset_flat) + listed_at(theirs[:entries], theirs[entries:])
    )
    ids = jnp.arange(all_blocks)
    below = ids < first
    prods = prods.reshape(block_count + 1, DH, head_count, DH).transpose(0, 2, 1, 3)
    previous, cumulative = prods[:-1], prods[1:]
    units_all = units.reshape(all_blocks, head_count, DH).transpose(1, 0, 2)
    k_all = kmat.reshape(all_blocks, head_count, DH).transpose(1, 0, 2)
    house_heads = house_dirs.reshape(block_count, head_count, DH)
    lengths = jnp.sqrt(jnp.sum(house_heads * house_heads, axis=-1, keepdims=True) + 1e-06)
    unit_dirs = house_heads / lengths
    query_f32 = query_rows.astype(jnp.float32).reshape(block_count, BLK, head_count, DH)
    key_f32 = key_rows.astype(jnp.float32).reshape(block_count, BLK, head_count, DH)
    back = collect(table, parts)
    dk_rot = (blocked(dk_local) + back[0]).reshape(block_count, BLK, head_count, DH)
    dv_out = (blocked(dv_local) + back[1]).astype(jnp.bfloat16).reshape(tok_rows, row_width)
    dq_rot = dq_rot.reshape(block_count, BLK, head_count, DH)
    dq_out = (
        jnp.einsum("bthm,bhnm->bthn", dq_rot, cumulative, precision=HIGH)
        .astype(jnp.bfloat16)
        .reshape(tok_rows, row_width)
    )
    dk_out = (
        jnp.einsum("bthm,bhnm->bthn", dk_rot, cumulative, precision=HIGH)
        .astype(jnp.bfloat16)
        .reshape(tok_rows, row_width)
    )
    dcum = jnp.einsum("bthn,bthm->bhnm", query_f32, dq_rot, precision=HIGH)
    dcum = dcum + jnp.einsum("bthn,bthm->bhnm", key_f32, dk_rot, precision=HIGH)

    carry = jnp.zeros((head_count, DH, DH), jnp.float32)
    adjoints = [None] * block_count
    for block in range(block_count - 1, -1, -1):
        adjoints[block] = dcum[block] + carry
        carry = reflect_apply(unit_dirs[block], adjoints[block])
    held = below[None, :, None].astype(jnp.float32)
    units_below = units_all * held
    k_below = k_all * held
    through = jnp.einsum("hin,hnm->him", units_below, carry, precision=HIGH)
    to_z = 0.5 * jnp.einsum("hib,him->hbm", solve, through, precision=HIGH)
    crossed = jnp.einsum("hbm,him->hbi", k_below, through, precision=HIGH)
    crossed = jnp.einsum("hbj,hji->hbi", crossed, solve, precision=HIGH)
    crossed = jnp.where(ids[:, None] < ids[None, :], crossed, 0.0)
    to_y = jnp.einsum("hbm,hnm->hbn", k_below, carry, precision=HIGH) - jnp.einsum(
        "hbi,hin->hbn", crossed, units_all, precision=HIGH
    )
    sent = jnp.stack([to_y, to_z], axis=0).transpose(2, 0, 1, 3).reshape(all_blocks, 4 * DH)
    came = lax.all_to_all(
        sent.reshape(ctx_count, block_count, 4 * DH), "ctx", split_axis=0, concat_axis=0, tiled=True
    )
    came = jnp.sum(came, axis=0).reshape(block_count, 2, head_count, DH)
    adjoint = jnp.stack(adjoints)
    k_own = lax.dynamic_slice_in_dim(k_all, first, block_count, axis=1)
    y_own = came[:, 0] + jnp.einsum("bhnm,hbm->bhn", adjoint, k_own, precision=HIGH)
    z_own = came[:, 1] + jnp.einsum("bhnm,bhn->bhm", adjoint, unit_dirs, precision=HIGH)
    dunit = -2.0 * (0.5 * y_own + jnp.einsum("bhnm,bhm->bhn", previous, z_own, precision=HIGH))
    house_grad = (dunit - unit_dirs * jnp.sum(unit_dirs * dunit, axis=-1, keepdims=True)) / lengths
    house_grad = house_grad.reshape(block_count, row_width)
    summed = jnp.zeros((w_query.shape[0], tok_rows), jnp.float32)
    for weight_mat, grad_mat in ((w_query, dq_out), (w_key, dk_out), (w_value, dv_out)):
        summed = summed + lax.dot_general(
            weight_mat, grad_mat, (((1,), (1,)), ((), ())), preferred_element_type=jnp.float32
        )
    share = lax.psum_scatter(
        summed.astype(jnp.bfloat16), "head", scatter_dimension=0, tiled=True
    ).astype(jnp.float32)
    return (share.T.astype(jnp.bfloat16), house_grad)


def solution(mesh):
    placed = (
        P("ctx", "head"),
        P("ctx", "head"),
        P("ctx", "head"),
        P("ctx", "head"),
        P("ctx", "head"),
        P("ctx", None),
        P("ctx", None),
        P(None, "head"),
        P(None, "head"),
        P(None, "head"),
    )
    return jax.shard_map(
        shards,
        mesh=mesh,
        in_specs=placed,
        out_specs=(P("ctx", "head"), P("ctx", "head")),
        check_vma=False,
    )
```
